32 devices in a mesh: dp: 4 (over z), fsdp: 8 (over y, x, core).
Axes of the slice: x: 2, y: 2, z: 4, core: 2. Of those that a mesh axis runs over, the one named last changes fastest.
Arguments:
- tokens: bfloat16 [12288, 1536], P(('dp', 'fsdp')), may hold values from -6 to 6
- cotangent: bfloat16 [12288, 1536], P(('dp', 'fsdp')), may hold values from -6 to 6
- segments: int32 [12288], P(('dp', 'fsdp')), may hold values from -1 to 7, as said below
- attn_gain: bfloat16 [1536], P('fsdp'), may hold values from 0.5 to 1.5
- query_weight: bfloat16 [1536, 1536], P('fsdp'), may hold values from -0.15625 to 0.15625
- query_bias: bfloat16 [1536], P('fsdp'), may hold values from -4 to 4
- key_weight: bfloat16 [1536, 256], P('fsdp'), may hold values from -0.15625 to 0.15625
- key_bias: bfloat16 [256], P('fsdp'), may hold values from -4 to 4
- value_weight: bfloat16 [1536, 256], P('fsdp'), may hold values from -0.15625 to 0.15625
- value_bias: bfloat16 [256], P('fsdp'), may hold values from -4 to 4
- out_weight: bfloat16 [1536, 1536], P('fsdp'), may hold values from -0.4375 to 0.4375
- ffn_gain: bfloat16 [1536], P('fsdp'), may hold values from 0.5 to 1.5
- gate_weight: bfloat16 [1536, 8960], P('fsdp'), may hold values from -0.15625 to 0.15625
- up_weight: bfloat16 [1536, 8960], P('fsdp'), may hold values from -0.15625 to 0.15625
- down_weight: bfloat16 [8960, 1536], P('fsdp'), may hold values from -0.0625 to 0.0625
Outputs:
- mixed: bfloat16 [12288, 1536], P(('dp', 'fsdp'))
- token_grad: float32 [12288, 1536], P(('dp', 'fsdp'))
- attn_gain_grad: float32 [1536], P('fsdp')
- query_weight_grad: float32 [1536, 1536], P('fsdp')
- query_bias_grad: float32 [1536], P('fsdp')
- key_weight_grad: float32 [1536, 256], P('fsdp')
- key_bias_grad: float32 [256], P('fsdp')
- value_weight_grad: float32 [1536, 256], P('fsdp')
- value_bias_grad: float32 [256], P('fsdp')
- out_weight_grad: float32 [1536, 1536], P('fsdp')
- ffn_gain_grad: float32 [1536], P('fsdp')
- gate_weight_grad: float32 [1536, 8960], P('fsdp')
- up_weight_grad: float32 [1536, 8960], P('fsdp')
- down_weight_grad: float32 [8960, 1536], P('fsdp')
The draws below stay inside these ranges and needn't reach their ends.
Inputs may be any that keep to these rules, and one draw needn't show every extreme that they name: `segments`: in each aligned block of 192 slots the live slots come first, at least 96 of them, numbered by sequence from 0 upward and never falling, at most 8 sequences a block; the rest are -1. The first block is one sequence of 192 slots; every other block has some empty slots.
All inputs are finite; a program needn't handle non-finite values.
Results may differ from the reference program's by a relative error of at most 0.028.
Values may be sent and summed in bfloat16 or wider, within the bound.
No kernel may reach another device: no remote copies, remote signals or barrier semaphores. Data moves between devices by JAX's collectives and lax.ppermute only.
A program may use at most 384 MiB of HBM per device.

```python
import jax
import jax.numpy as jnp
from jax import lax

D = 1536
HEADS = 12
KV_HEADS = 2
HD = 128
FF = 8960
MB_TOK = 192
TOKENS = 12288


def draw_segments(key, part):
    blocks = TOKENS // MB_TOK
    first_key = jax.random.fold_in(key, 11)
    second_key = jax.random.fold_in(key, 23)
    starts = jax.random.randint(first_key, (blocks, MB_TOK), 0, MB_TOK // 2) == 0
    positions = jnp.arange(MB_TOK, dtype=jnp.int32)[None, :]
    rows = jnp.arange(blocks, dtype=jnp.int32)[:, None]
    step_size = MB_TOK // 16
    forced = (rows == 1) & (positions % step_size == 0) & (positions < 8 * step_size)
    starts = starts | (positions == 0) | forced
    numbers = jnp.minimum(jnp.cumsum(starts.astype(jnp.int32), axis=1) - 1, 7)
    filled = jax.random.randint(second_key, (blocks, 1), MB_TOK // 2, MB_TOK)
    leading = rows == 0
    numbers = jnp.where(leading, 0, numbers)
    filled = jnp.where(leading, MB_TOK, filled)
    numbers = jnp.where(positions < filled, numbers, -1)
    return numbers.reshape(TOKENS).astype(jnp.int32)


def steps_of(stream_key, extent, shards, smallest, high):
    loudness, own = 1.0, jax.random.fold_in(stream_key, 6)
    for dim, parts in shards:
        steps = jnp.exp(jax.random.uniform(jax.random.fold_in(own, dim), (parts,), jnp.float32, smallest / len(shards), high / len(shards)))
        loudness = loudness * jnp.repeat(steps, extent[dim] // parts).reshape([-1 if axis == dim else 1 for axis in range(len(extent))])
    return loudness


def noise(key, shape, deviation, most, cuts=(), kind=jnp.bfloat16):
    entries = deviation * jax.random.normal(key, shape, jnp.float32)
    if cuts:
        entries = entries * steps_of(key, shape, cuts, -0.22, 0.18)
    return jnp.clip(entries, -most, most).astype(kind)


def setup_inputs(seed: int = 0) -> dict:
    arg_keys = jax.random.split(jax.random.key(seed), 16)
    return {
        "tokens": noise(arg_keys[0], (TOKENS, D), 1.0, 6.0, ((0, 32),)),
        "cotangent": noise(arg_keys[1], (TOKENS, D), 1.0, 6.0, ((0, 32),)),
        "segments": draw_segments(jax.random.fold_in(arg_keys[15], 71), 0),
        "attn_gain": jnp.clip(1.0 + 0.1 * jax.random.normal(arg_keys[3], (D,), jnp.float32), 0.5, 1.5).astype(jnp.bfloat16),
        "query_weight": noise(arg_keys[4], (D, D), D ** -0.5, 0.15625, ((0, 8),)),
        "query_bias": noise(arg_keys[5], (D,), 1.0, 4.0, ((0, 8),)),
        "key_weight": noise(arg_keys[6], (D, KV_HEADS * HD), D ** -0.5, 0.15625, ((0, 8),)),
        "key_bias": noise(arg_keys[7], (KV_HEADS * HD,), 1.0, 4.0, ((0, 8),)),
        "value_weight": noise(arg_keys[8], (D, KV_HEADS * HD), D ** -0.5, 0.15625, ((0, 8),)),
        "value_bias": noise(arg_keys[9], (KV_HEADS * HD,), 1.0, 4.0, ((0, 8),)),
        "out_weight": noise(arg_keys[10], (D, D), (D // 8) ** -0.5, 0.4375, ((0, 8),)),
        "ffn_gain": jnp.clip(1.0 + 0.1 * jax.random.normal(arg_keys[11], (D,), jnp.float32), 0.5, 1.5).astype(jnp.bfloat16),
        "gate_weight": noise(arg_keys[12], (D, FF), D ** -0.5, 0.15625, ((0, 8),)),
        "up_weight": noise(arg_keys[13], (D, FF), D ** -0.5, 0.15625, ((0, 8),)),
        "down_weight": noise(arg_keys[14], (FF, D), FF ** -0.5, 0.0625, ((0, 8),)),
    }


@jax.custom_vjp
def low(v):
    return lax.optimization_barrier(v.astype(jnp.bfloat16)).astype(jnp.float32)

@jax.custom_vjp
def low_back(v):
    return v

def low_keep(v):
    return (low(v), None)

def low_pass(kept, grad):
    return (grad,)

def back_keep(v):
    return (v, None)

def back_low(kept, grad):
    return (low(grad),)
low.defvjp(low_keep, low_pass)
low_back.defvjp(back_keep, back_low)
NORM_EPS = 1e-06
ROPE_BASE = 1000000.0
MASKED = -1e+30

def highest(left_side, right_side):
    return jnp.dot(left_side, right_side, precision=lax.Precision.HIGHEST)

def rope_tables(seg_block):
    length_rows = seg_block.shape[0]
    positions = jnp.arange(length_rows, dtype=jnp.int32)
    previous = jnp.concatenate([seg_block[:1] - 1, seg_block[:-1]])
    begins = lax.cummax(jnp.where(seg_block != previous, positions, 0), axis=0)
    offsets = (positions - begins).astype(jnp.float32)
    halves = HD // 2
    inverse = ROPE_BASE ** (-(jnp.arange(halves, dtype=jnp.float32) * (2.0 / HD)))
    angles = offsets[:, None] * inverse[None, :]
    return (jnp.cos(angles), jnp.sin(angles))

def rotate(inputs, cosine, sine_table):
    halves = inputs.shape[-1] // 2
    leading = inputs[..., :halves]
    trailing = inputs[..., halves:]
    return jnp.concatenate([leading * cosine - trailing * sine_table, trailing * cosine + leading * sine_table], axis=-1)

def rms_unit(inputs):
    return inputs * lax.rsqrt(lax.optimization_barrier(jnp.mean(inputs * inputs, axis=-1, keepdims=True)) + NORM_EPS)

def block_forward(params, inputs, seg_block):
    attn_gain, query_weight, query_bias, key_weight, key_bias, value_weight, value_bias, out_weight, ffn_gain, gate_weight, up_weight, down_weight = params
    row_count = inputs.shape[0]
    groups = HEADS // KV_HEADS
    cosine, sine_table = rope_tables(seg_block)
    cosine = cosine[:, None, :]
    sine_table = sine_table[:, None, :]
    normed = low(rms_unit(inputs) * attn_gain)
    query_lin = low_back(highest(normed, query_weight) + query_bias)
    key_lin = low_back(highest(normed, key_weight) + key_bias)
    value_lin = low(low_back(highest(normed, value_weight) + value_bias))
    query_rot = low(rotate(query_lin.reshape(row_count, HEADS, HD), cosine, sine_table))
    query_rot = query_rot.reshape(row_count, KV_HEADS, groups, HD)
    key_rot = low(rotate(key_lin.reshape(row_count, KV_HEADS, HD), cosine, sine_table))
    value_heads = value_lin.reshape(row_count, KV_HEADS, HD)
    scores = jnp.einsum('ighd,jgd->ghij', query_rot, key_rot, precision=lax.Precision.HIGHEST) * HD ** (-0.5)
    scores = low_back(scores)
    positions = jnp.arange(row_count, dtype=jnp.int32)
    allowed = (seg_block[:, None] == seg_block[None, :]) & (positions[None, :] <= positions[:, None])
    weights = jax.nn.softmax(jnp.where(allowed[None, None], scores, MASKED), axis=-1)
    attended = jnp.einsum('ghij,jgd->ighd', low(weights), value_heads, precision=lax.Precision.HIGHEST)
    attended = low(low_back(attended.reshape(row_count, HEADS * HD)))
    middle = inputs + low_back(highest(attended, out_weight))
    normed_ffn = low(rms_unit(middle) * ffn_gain)
    gate_lin = low_back(highest(normed_ffn, gate_weight))
    upward = low_back(highest(normed_ffn, up_weight))
    hidden = low(jax.nn.silu(gate_lin) * upward)
    return middle + low_back(highest(hidden, down_weight))

def reference(tokens, cotangent, segments, attn_gain, query_weight, query_bias, key_weight, key_bias, value_weight, value_bias, out_weight, ffn_gain, gate_weight, up_weight, down_weight):
    params = tuple((member.astype(jnp.float32) for member in (attn_gain, query_weight, query_bias, key_weight, key_bias, value_weight, value_bias, out_weight, ffn_gain, gate_weight, up_weight, down_weight)))
    slot_total = segments.shape[0]
    blocks = slot_total // MB_TOK
    inputs = tokens.astype(jnp.float32).reshape(blocks, MB_TOK, D)
    seg_blocks = segments.reshape(blocks, MB_TOK)
    live_rows = (segments >= 0).astype(jnp.float32)[:, None]
    seed_grad = (cotangent.astype(jnp.float32) * live_rows).reshape(blocks, MB_TOK, D)

    def whole_layer(param_set, token_set):

        def one_block(pieces):
            return jax.checkpoint(block_forward)(param_set, pieces[0], pieces[1])
        return lax.map(one_block, (token_set, seg_blocks))
    mixed, pullback = jax.vjp(whole_layer, params, inputs)
    param_grads, token_grads = pullback(seed_grad)
    return (mixed.reshape(slot_total, D).astype(jnp.bfloat16), token_grads.reshape(slot_total, D), param_grads[0], param_grads[1], param_grads[2], param_grads[3], param_grads[4], param_grads[5], param_grads[6], param_grads[7], param_grads[8], param_grads[9], param_grads[10], param_grads[11])
```

```python
import jax
import jax.numpy as jnp
from jax import lax
from jax.sharding import PartitionSpec as P

HEADS = 12
KV_HEADS = 2
GROUPS = HEADS // KV_HEADS
HD = 128
MB_TOK = 192
NORM_EPS = 1e-06
ROPE_BASE = 1000000.0
MASKED = -1e30
SLOTS = (0, 2, 4, 6, 1, 3, 5, 7)
BF = jnp.bfloat16
F32 = jnp.float32


def mm(a, b):
    return jnp.dot(a, b, preferred_element_type=F32)


def mm_t(a, b):
    return lax.dot_general(a, b, (((1,), (1,)), ((), ())), preferred_element_type=F32)


def t_mm(a, b):
    return lax.dot_general(a, b, (((0,), (0,)), ((), ())), preferred_element_type=F32)


def plus(*terms):
    total = terms[0].astype(F32)
    for term in terms[1:]:
        total = total + term.astype(F32)
    return total


def at(stack, index):
    return lax.dynamic_index_in_dim(stack, index, 0, keepdims=False)


class Group:
    def __init__(self, size):
        self.size = size
        self.me = lax.axis_index("fsdp")
        self.hand = size == 8

    def hop(self, value, step):
        return lax.ppermute(value, "fsdp", [(i, i ^ step) for i in range(self.size)])

    def spread(self, piece):
        half = piece.shape[0] // 2
        own = {0: piece}
        own[2] = self.hop(piece, 2)
        own[4] = self.hop(piece, 4)
        six = [self.hop(own[4][:half], 2), self.hop(own[2][half:], 4)]
        got = {s: [own[s]] for s in (0, 2, 4)}
        got[6] = six
        for s in (0, 2, 4, 6):
            got[s ^ 1] = [self.hop(part, 1) for part in got[s]]
        return got

    def gather_tokens(self, rows):
        if not self.hand:
            return lax.all_gather(rows, "fsdp", axis=0, tiled=True)
        got = self.spread(rows)
        return jnp.concatenate([part for s in SLOTS for part in got[s]], axis=0)

    def gather_rows(self, rows):
        if not self.hand:
            return lax.all_gather(rows, "fsdp", axis=0, tiled=True)
        got = self.spread(rows)
        count = rows.shape[0]
        whole = jnp.zeros((self.size * count,) + rows.shape[1:], rows.dtype)
        for s in SLOTS:
            start = (self.me ^ s) * count
            for part in got[s]:
                whole = lax.dynamic_update_slice_in_dim(whole, part, start, 0)
                start = start + part.shape[0]
        return whole

    def reduce_slots(self, mine, theirs):
        low = lambda v: v.astype(BF)
        got = self.hop(theirs(), 1)
        part = [low(plus(mine(i), got[i] if i.__class__ is int else at(got, i))) for i in self.order]
        half = part[0].shape[0] // 2
        first, across, up, far = part
        far_across = self.hop(far[:half], 2)
        far_up = self.hop(far[half:], 4)
        across_low = self.hop(across[:half], 2)
        up_high = self.hop(up[half:], 4)
        up_low = self.hop(low(plus(up[:half], far_across)), 4)
        across_high = self.hop(low(plus(across[half:], far_up)), 2)
        return jnp.concatenate(
            [plus(first[:half], across_low, up_low), plus(first[half:], across_high, up_high)], axis=0
        )

    def scatter_tokens(self, sums):
        if not self.hand:
            return lax.psum_scatter(sums, "fsdp", scatter_dimension=0, tiled=True).astype(F32)
        stack = sums.reshape(2, 4, sums.shape[0] // 8, sums.shape[1])
        self.order = (0, 1, 2, 3)
        return self.reduce_slots(lambda i: stack[0, i], lambda: stack[1])

    def scatter_rows(self, sums):
        if not self.hand:
            return lax.psum_scatter(sums, "fsdp", scatter_dimension=0, tiled=True).astype(F32)
        stack = sums.reshape(4, 2, sums.shape[0] // 8, sums.shape[1])
        core, chip = self.me & 1, self.me >> 1
        mine = lax.dynamic_index_in_dim(stack, core, 1, keepdims=False)
        self.order = (chip, chip ^ 1, chip ^ 2, chip ^ 3)
        return self.reduce_slots(
            lambda i: at(mine, i), lambda: lax.dynamic_index_in_dim(stack, 1 - core, 1, keepdims=False)
        )

    def exchange(self, stack):
        if not self.hand:
            return lax.all_to_all(stack, "fsdp", split_axis=0, concat_axis=0, tiled=True)
        return [at(stack, self.me)] + [self.hop(at(stack, self.me ^ s), s) for s in range(1, 8)]

    def place(self, got):
        if not self.hand:
            return got
        stack = jnp.zeros((8,) + got[0].shape, got[0].dtype)
        for s in range(8):
            stack = lax.dynamic_update_index_in_dim(stack, got[s], self.me ^ s, 0)
        return stack

    def gather_small(self, vector):
        if not self.hand:
            return lax.all_gather(vector, "fsdp", axis=0, tiled=False)
        stack = jnp.zeros((8,) + vector.shape, vector.dtype)
        got = {0: vector}
        for step in (1, 2, 4):
            for s in list(got):
                got[s ^ step] = self.hop(got[s], step)
        for s in range(8):
            stack = lax.dynamic_update_index_in_dim(stack, got[s], self.me ^ s, 0)
        return stack

    def sum_small(self, vector):
        if not self.hand:
            return lax.psum(vector, "fsdp")
        for step in (1, 2, 4):
            vector = vector + self.hop(vector, step)
        return vector


def chain(parts, size):
    count = parts.shape[0]
    z = lax.axis_index("dp")
    flow = {}
    for name, rank, perm in (
        ("up", z, [(i, i + 1) for i in range(size - 1)]),
        ("down", size - 1 - z, [(i + 1, i) for i in range(size - 1)]),
    ):
        got = []
        for step in range(count + size - 2):
            item = at(parts, jnp.clip(step - rank, 0, count - 1))
            if got:
                item = plus(item, got[-1]).astype(BF)
            got.append(lax.ppermute(item, "dp", perm))
        flow[name] = (rank, got)
    sums = []
    for c in range(count):
        total = parts[c].astype(F32)
        for rank, got in flow.values():
            come = got[c]
            for r in range(2, size):
                come = jnp.where(rank == r, got[c + r - 1], come)
            total = total + come.astype(F32)
        sums.append(total)
    return sums


def rope_tables(segs):
    blocks, length = segs.shape
    positions = jnp.arange(length, dtype=jnp.int32)[None, :]
    previous = jnp.concatenate([segs[:, :1] - 1, segs[:, :-1]], axis=1)
    begins = lax.cummax(jnp.where(segs != previous, positions, 0), axis=1)
    offsets = (positions - begins).astype(F32)
    halves = HD // 2
    inverse = ROPE_BASE ** (-(jnp.arange(halves, dtype=F32) * (2.0 / HD)))
    angles = offsets.reshape(-1)[:, None] * inverse[None, :]
    return jnp.cos(angles)[:, None, :], jnp.sin(angles)[:, None, :]


def rotate(inputs, cosine, sine):
    halves = HD // 2
    a, b = inputs[..., :halves], inputs[..., halves:]
    return jnp.concatenate([a * cosine - b * sine, b * cosine + a * sine], axis=-1)


def norm_back(grad_unit, unit_rows, recip_rows):
    return recip_rows * (
        grad_unit - unit_rows * jnp.mean(grad_unit * unit_rows, axis=-1, keepdims=True)
    )


def local(
    tokens,
    cotangent,
    segments,
    attn_gain,
    query_weight,
    query_bias,
    key_weight,
    key_bias,
    value_weight,
    value_bias,
    out_weight,
    ffn_gain,
    gate_weight,
    up_weight,
    down_weight,
    fsdp,
    dp,
):
    group = Group(fsdp)
    rows, width = tokens.shape
    blocks = rows // MB_TOK
    kv_width = KV_HEADS * HD
    shard, ff = gate_weight.shape
    part_ff = ff // fsdp

    small = jnp.concatenate([attn_gain, ffn_gain, query_bias, key_bias, value_bias])
    small = group.gather_small(small)
    cuts = [shard, 2 * shard, 3 * shard, 3 * shard + kv_width // fsdp]
    attn_gain, ffn_gain, query_bias, key_bias, value_bias = (
        piece.reshape(-1).astype(F32) for piece in jnp.split(small, cuts, axis=1)
    )
    qkv_bias = jnp.concatenate([query_bias, key_bias, value_bias])
    qkv = group.gather_rows(jnp.concatenate([query_weight, key_weight, value_weight], axis=1))
    out = group.gather_rows(out_weight)

    segs = segments.reshape(blocks, MB_TOK)
    live = (segments >= 0).astype(F32)[:, None]
    seed = cotangent.astype(F32) * live
    seed_all = group.gather_tokens(seed.astype(BF))

    def columns(weight):
        stack = weight.reshape(shard, fsdp, part_ff).transpose(1, 0, 2)
        return group.place(group.exchange(stack)).reshape(fsdp * shard, part_ff)

    gate = columns(gate_weight)
    upw = columns(up_weight)

    cosine, sine = rope_tables(segs)
    x = tokens.astype(F32)
    recip_attn = lax.rsqrt(jnp.mean(x * x, axis=-1, keepdims=True) + NORM_EPS)
    unit_attn = x * recip_attn
    normed = (unit_attn * attn_gain).astype(BF)
    lin = mm(normed, qkv) + qkv_bias
    query_rot = rotate(lin[:, :width].reshape(rows, HEADS, HD), cosine, sine).astype(BF)
    query_rot = query_rot.reshape(blocks, MB_TOK, KV_HEADS, GROUPS, HD)
    key_rot = rotate(lin[:, width : width + kv_width].reshape(rows, KV_HEADS, HD), cosine, sine)
    key_rot = key_rot.astype(BF).reshape(blocks, MB_TOK, KV_HEADS, HD)
    value = lin[:, width + kv_width :].astype(BF).reshape(blocks, MB_TOK, KV_HEADS, HD)
    positions = jnp.arange(MB_TOK, dtype=jnp.int32)
    allowed = (segs[:, :, None] == segs[:, None, :]) & (positions[None, :] <= positions[:, None])
    scores = jnp.einsum("mighd,mjgd->mghij", query_rot, key_rot, preferred_element_type=F32)
    scores = jnp.where(allowed[:, None, None], scores * HD ** (-0.5), MASKED)
    exponent = jnp.exp(scores - jnp.max(scores, axis=-1, keepdims=True))
    probs = exponent / jnp.sum(exponent, axis=-1, keepdims=True)
    probs_low = probs.astype(BF)
    attended = jnp.einsum("mghij,mjgd->mighd", probs_low, value, preferred_element_type=F32)
    attended = attended.reshape(rows, HEADS * HD).astype(BF)
    middle = x + mm(attended, out)
    recip_ffn = lax.rsqrt(jnp.mean(middle * middle, axis=-1, keepdims=True) + NORM_EPS)
    unit_ffn = middle * recip_ffn
    normed_ffn = (unit_ffn * ffn_gain).astype(BF)

    normed_all = group.gather_tokens(normed_ffn)
    gate_lin = mm(normed_all, gate)
    upward = mm(normed_all, upw)
    sigmoid = jax.nn.sigmoid(gate_lin)
    hidden = (gate_lin * sigmoid * upward).astype(BF)
    grad_hidden = mm_t(seed_all, down_weight)
    grad_gate = (grad_hidden * upward * sigmoid * (1.0 + gate_lin * (1.0 - sigmoid))).astype(BF)
    grad_up = (grad_hidden * (gate_lin * sigmoid)).astype(BF)
    grad_normed_ffn = group.scatter_tokens(
        (mm_t(grad_gate, gate) + mm_t(grad_up, upw)).astype(BF)
    )
    down_part = t_mm(hidden, seed_all).astype(BF)
    down_cut = 7 if part_ff % 56 == 0 else 1
    down_sum = chain(down_part.reshape(down_cut, part_ff // down_cut, width), dp)
    down_sum = jnp.concatenate(down_sum, axis=0)

    def owned(grad):
        stack = t_mm(normed_all, grad).astype(BF).reshape(fsdp, shard, part_ff)
        got = group.exchange(stack)
        got = jnp.stack(got) if group.hand else got
        sums = jnp.stack(chain(got, dp))
        if group.hand:
            sums = [at(sums, group.me ^ j) for j in range(fsdp)]
        else:
            sums = [sums[j] for j in range(fsdp)]
        return jnp.concatenate(sums, axis=1)

    gate_sum = owned(grad_gate)
    up_sum = owned(grad_up)
    mixed = (middle + group.scatter_tokens(mm(hidden, down_weight).astype(BF))).astype(BF)

    grad_middle = seed + norm_back(grad_normed_ffn * ffn_gain, unit_ffn, recip_ffn)
    grad_branch = grad_middle.astype(BF)
    row_cut = 6 if shard % 48 == 0 else 1

    def own_rows(left, right):
        sums = group.scatter_rows(t_mm(left, right).astype(BF)).astype(BF)
        sums = chain(sums.reshape(row_cut, shard // row_cut, sums.shape[1]), dp)
        return jnp.concatenate(sums, axis=0)

    out_sum = own_rows(attended, grad_branch)
    grad_attended = mm_t(grad_branch, out).astype(BF)
    grad_attended = grad_attended.reshape(blocks, MB_TOK, KV_HEADS, GROUPS, HD)
    grad_probs = jnp.einsum("mighd,mjgd->mghij", grad_attended, value, preferred_element_type=F32)
    grad_value = jnp.einsum("mghij,mighd->mjgd", probs_low, grad_attended, preferred_element_type=F32)
    inner = jnp.sum(grad_probs * probs, axis=-1, keepdims=True)
    grad_scores = (probs * (grad_probs - inner)).astype(BF)
    grad_query = jnp.einsum("mghij,mjgd->mighd", grad_scores, key_rot, preferred_element_type=F32)
    grad_key = jnp.einsum("mghij,mighd->mjgd", grad_scores, query_rot, preferred_element_type=F32)
    scale = HD ** (-0.5)
    grad_query = rotate(grad_query.reshape(rows, HEADS, HD) * scale, cosine, -sine)
    grad_key = rotate(grad_key.reshape(rows, KV_HEADS, HD) * scale, cosine, -sine)
    grad_lin = jnp.concatenate(
        [
            grad_query.reshape(rows, width).astype(BF),
            grad_key.reshape(rows, kv_width).astype(BF),
            grad_value.reshape(rows, kv_width).astype(BF),
        ],
        axis=1,
    )
    qkv_sum = own_rows(normed, grad_lin)
    grad_normed = mm_t(grad_lin, qkv)
    token_grad = grad_middle + norm_back(grad_normed * attn_gain, unit_attn, recip_attn)

    terms = jnp.concatenate(
        [
            jnp.sum(grad_normed * unit_attn, axis=0),
            jnp.sum(grad_normed_ffn * unit_ffn, axis=0),
            jnp.sum(grad_lin.astype(F32), axis=0),
        ]
    )
    terms = group.sum_small(terms)
    for step in (1, 2):
        terms = terms + lax.ppermute(terms, "dp", [(i, i ^ step) for i in range(dp)]) if dp == 4 else terms
    if dp != 4:
        terms = lax.psum(terms, "dp")

    def mine(start, size):
        count = size // fsdp
        return lax.dynamic_slice_in_dim(terms, start + group.me * count, count, 0)

    return (
        mixed,
        token_grad,
        mine(0, width),
        qkv_sum[:, :width],
        mine(2 * width, width),
        qkv_sum[:, width : width + kv_width],
        mine(3 * width, kv_width),
        qkv_sum[:, width + kv_width :],
        mine(3 * width + kv_width, kv_width),
        out_sum,
        mine(width, width),
        gate_sum,
        up_sum,
        down_sum,
    )


def solution(mesh):
    fsdp, dp = mesh.shape["fsdp"], mesh.shape["dp"]
    tok, vec, mat = P(("dp", "fsdp"), None), P("fsdp"), P("fsdp", None)
    return jax.shard_map(
        lambda *args: local(*args, fsdp, dp),
        mesh=mesh,
        in_specs=(tok, tok, P(("dp", "fsdp")), vec, mat, vec, mat, vec, mat, vec, mat, vec, mat, mat, mat),
        out_specs=(tok, tok, vec, mat, vec, mat, vec, mat, vec, mat, vec, mat, mat, mat),
        check_vma=False,
    )
```
